32 devices in a mesh: wide: 8 (over y, x, core), narrow: 4 (over z).
Axes of the slice: x: 2, y: 2, z: 4, core: 2. Of those that a mesh axis runs over, the one named last changes fastest.
Arguments:
- velocity: float32 [3, 64, 32, 128], P(None, 'wide', 'narrow'), may hold values from -6 to 6
- force: float32 [3, 64, 32, 128], P(None, 'wide', 'narrow'), may hold values from -6 to 6
- visc_class: int32 [64, 32, 128], P('wide', 'narrow'), may hold values from 0 to 3
- visc_table: float32 [4], replicated, may hold values from 0.2 to 5
- multiplier: float32 [3, 64, 2048], P(None, ('wide', 'narrow')), may hold values from -6 to 6
- marker_cell: int32 [64, 2048], P(('wide', 'narrow')), may hold values from 0 to 8190, as said below
- marker_frac: float32 [3, 64, 2048], P(None, ('wide', 'narrow')), may hold values from 0 to 1
- pair_sphere: int32 [1024], P(('wide', 'narrow')), may hold values from 0 to 1
- pair_partner: int32 [1024], P(('wide', 'narrow')), may hold values from 0 to 17
- pair_normal: float32 [3, 1024], P(None, ('wide', 'narrow')), may hold values from -6 to 6
- pair_gap: float32 [1024], P(('wide', 'narrow')), may hold values from -6 to 6
- contact_force: float32 [1024], P(('wide', 'narrow')), may hold values from 0 to 1
Outputs:
- fluid_velocity: float32 [3, 64, 32, 128], P(None, 'wide', 'narrow')
- rigid_multiplier: float32 [3, 64, 2048], P(None, ('wide', 'narrow'))
- contact_multiplier: float32 [1024], P(('wide', 'narrow'))
The draws below stay inside these ranges and needn't reach their ends.
Inputs may be any that keep to these rules, and one draw needn't show every extreme that they name: marker_cell[s, m] = (i * 8 + j) * 128 + k for a cell (i, j, k) of the brick that owns sphere s, with k <= 126; the markers of one sphere lie within a few cells of each other.
All inputs are finite; a program needn't handle non-finite values.
Results may differ from the reference program's by a relative error of at most 0.0003.
Values sent between devices are 32-bit elements; how exact they have to be, the bound alone decides.
No kernel may reach another device: no remote copies, remote signals or barrier semaphores. Data moves between devices by JAX's collectives and lax.ppermute only.
A program may use at most 64 MiB of HBM per device.

```python
import math
import jax
import jax.numpy as jnp

CX = 8
CY = 8
NZ = 128
SPH_DEV = 2
MARK = 2048
PAIRS_DEV = 32
NVISC = 4
ITERS = 2
SWEEPS = 2
NX = 64
NY = 32
SPHERES = 64
PAIRS = 1024
N_WIDE = 8
N_NARROW = 4


def draw_marker_cell(key, part):
    keys = jax.random.split(jax.random.fold_in(key, 11), 6)
    centre_x = jax.random.randint(keys[0], (SPHERES, 1), 0, CX)
    centre_y = jax.random.randint(keys[1], (SPHERES, 1), 0, CY)
    centre_z = jax.random.randint(keys[2], (SPHERES, 1), 0, NZ - 1)
    cell_x = jnp.clip(centre_x + jax.random.randint(keys[3], (SPHERES, MARK), -4, 5), 0, CX - 1)
    cell_y = jnp.clip(centre_y + jax.random.randint(keys[4], (SPHERES, MARK), -4, 5), 0, CY - 1)
    cell_z = jnp.clip(centre_z + jax.random.randint(keys[5], (SPHERES, MARK), -4, 5), 0, NZ - 2)
    result = (cell_x * CY + cell_y) * NZ + cell_z
    result = result.at[0, 0].set(0)
    result = result.at[0, 1].set(CX * CY * NZ - 2)
    return result.astype(jnp.int32)


def set_ends(values, own_key, least, top_value):
    longest = values.shape.index(max(values.shape))
    spots = []
    for shift in (0, 1):
        where = [jax.random.randint(jax.random.fold_in(own_key, axis), (), 0, length) for axis, length in enumerate(values.shape)]
        where[longest] = (where[longest] + shift) % values.shape[longest]
        spots.append(tuple(where))
    return values.at[spots[0]].set(least).at[spots[1]].set(top_value)


def block_levels(own_key, dims, cuts, least, high):
    def one(position, shards_of):
        steps = jax.random.uniform(jax.random.fold_in(jax.random.fold_in(own_key, 6), position), (shards_of,), jnp.float32, least / len(cuts), high / len(cuts))
        return jnp.repeat(jnp.exp(steps), dims[position] // shards_of).reshape((-1,) + (1,) * (len(dims) - position - 1))

    level = one(*cuts[0])
    for cut in cuts[1:]:
        level = level * one(*cut)
    return level


def bell_draw(key, extent, spread, limit, cuts=(), kind=jnp.bfloat16):
    loudness = block_levels(key, extent, cuts, -0.22, 0.18) if cuts else 1.0
    array = jax.random.normal(key, extent, jnp.float32) * spread * loudness
    return jnp.minimum(jnp.maximum(array, -limit), limit).astype(kind)


def setup_inputs(seed: int = 0) -> dict:
    key_of = jax.random.split(jax.random.key(seed), 13)
    velocity = bell_draw(key_of[0], (3, NX, NY, NZ), 1.0, 6.0, ((1, 8), (2, 4)), jnp.float32)
    force = bell_draw(key_of[1], (3, NX, NY, NZ), 1.0, 6.0, ((1, 8), (2, 4)), jnp.float32)
    visc_class = set_ends(jax.random.randint(key_of[2], (NX, NY, NZ), 0, NVISC), jax.random.fold_in(key_of[2], 1), 0, NVISC - 1).astype(jnp.int32)
    visc_table = jnp.clip(jnp.exp(jax.random.uniform(key_of[3], (NVISC,), jnp.float32, math.log(0.2), math.log(5.0))), 0.2, 5.0)
    multiplier = bell_draw(key_of[4], (3, SPHERES, MARK), 1.0, 6.0, ((1, 32),), jnp.float32)
    marker_cell = draw_marker_cell(jax.random.fold_in(key_of[12], 71), 0)
    marker_frac = jnp.clip(1.0 * jax.random.uniform(key_of[6], (3, SPHERES, MARK), jnp.float32) ** block_levels(key_of[6], (3, SPHERES, MARK), ((1, 32),), -0.2, 0.2), 0.0, 1.0)
    pair_sphere = set_ends(jax.random.randint(key_of[7], (PAIRS,), 0, SPH_DEV), jax.random.fold_in(key_of[7], 1), 0, SPH_DEV - 1).astype(jnp.int32)
    pair_partner = set_ends(jax.random.randint(key_of[8], (PAIRS,), 0, 9 * SPH_DEV), jax.random.fold_in(key_of[8], 1), 0, (9 * SPH_DEV) - 1).astype(jnp.int32)
    pair_normal = bell_draw(key_of[9], (3, PAIRS), 1.0, 6.0, ((1, 32),), jnp.float32)
    pair_gap = bell_draw(key_of[10], (PAIRS,), 1.0, 6.0, ((0, 32),), jnp.float32)
    contact_force = jnp.clip(1.0 * jax.random.uniform(key_of[11], (PAIRS,), jnp.float32) ** block_levels(key_of[11], (PAIRS,), ((0, 32),), -0.2, 0.2), 0.0, 1.0)
    return {"velocity": velocity, "force": force, "visc_class": visc_class, "visc_table": visc_table, "multiplier": multiplier, "marker_cell": marker_cell, "marker_frac": marker_frac, "pair_sphere": pair_sphere, "pair_partner": pair_partner, "pair_normal": pair_normal, "pair_gap": pair_gap, "contact_force": contact_force}


base_diag = 1.0
spread_gain = 0.25
rigid_step = 0.5
contact_step = 0.5
contact_gain = 0.5


def reference(velocity, force, visc_class, visc_table, multiplier, marker_cell, marker_frac, pair_sphere, pair_partner, pair_normal, pair_gap, contact_force):
    classes = jnp.arange(NVISC, dtype=jnp.int32)
    viscosity = jnp.sum(jnp.where(visc_class[None] == classes[:, None, None, None], visc_table[:, None, None, None], jnp.float32(0.0)), axis=0)
    padded_mu = jnp.pad(viscosity, 1)
    face_coef = [
        0.5 * (viscosity + padded_mu[:-2, 1:-1, 1:-1]),
        0.5 * (viscosity + padded_mu[2:, 1:-1, 1:-1]),
        0.5 * (viscosity + padded_mu[1:-1, :-2, 1:-1]),
        0.5 * (viscosity + padded_mu[1:-1, 2:, 1:-1]),
        0.5 * (viscosity + padded_mu[1:-1, 1:-1, :-2]),
        0.5 * (viscosity + padded_mu[1:-1, 1:-1, 2:]),
    ]
    diagonal = base_diag + face_coef[0] + face_coef[1] + face_coef[2] + face_coef[3] + face_coef[4] + face_coef[5]

    owner = jnp.arange(SPHERES, dtype=jnp.int32) // SPH_DEV
    column = owner // N_NARROW
    row = owner % N_NARROW
    cell_x = marker_cell // (CY * NZ) + column[:, None] * CX
    cell_y = (marker_cell // NZ) % CY + row[:, None] * CY
    cell_z = marker_cell % NZ
    corner_list = []
    for step_x in (0, 1):
        for step_y in (0, 1):
            for step_z in (0, 1):
                index = ((cell_x + step_x) * (NY + 1) + cell_y + step_y) * NZ + cell_z + step_z
                weight_x = marker_frac[0] if step_x else 1.0 - marker_frac[0]
                weight_y = marker_frac[1] if step_y else 1.0 - marker_frac[1]
                weight_z = marker_frac[2] if step_z else 1.0 - marker_frac[2]
                corner_list.append((index.reshape(-1).astype(jnp.int32), (weight_x * weight_y * weight_z).reshape(-1)))

    pair_owner = jnp.arange(PAIRS, dtype=jnp.int32) // PAIRS_DEV
    pair_column = pair_owner // N_NARROW
    pair_row = pair_owner % N_NARROW
    own_index = pair_owner * SPH_DEV + pair_sphere
    block = pair_partner // SPH_DEV
    target_column = pair_column + block // 3 - 1
    target_row = pair_row + block % 3 - 1
    valid = (target_column >= 0) & (target_column < N_WIDE) & (target_row >= 0) & (target_row < N_NARROW)
    partner_index = (jnp.clip(target_column, 0, N_WIDE - 1) * N_NARROW + jnp.clip(target_row, 0, N_NARROW - 1)) * SPH_DEV + pair_partner % SPH_DEV

    for outer in range(ITERS):
        flat_mult = multiplier.reshape(3, -1)
        grid = jnp.zeros((3, (NX + 1) * (NY + 1) * NZ), jnp.float32)
        for index, weight in corner_list:
            grid = grid.at[:, index].add(spread_gain * flat_mult * weight[None])
        grid_force = grid.reshape(3, NX + 1, NY + 1, NZ)[:, :NX, :NY]
        rhs = force + grid_force
        for inner in range(SWEEPS):
            grown = jnp.pad(velocity, ((0, 0), (1, 1), (1, 1), (1, 1)))
            neighbour_sum = (face_coef[0] * grown[:, :-2, 1:-1, 1:-1] + face_coef[1] * grown[:, 2:, 1:-1, 1:-1]
                             + face_coef[2] * grown[:, 1:-1, :-2, 1:-1] + face_coef[3] * grown[:, 1:-1, 2:, 1:-1]
                             + face_coef[4] * grown[:, 1:-1, 1:-1, :-2] + face_coef[5] * grown[:, 1:-1, 1:-1, 2:])
            velocity = (rhs + neighbour_sum) / diagonal
        flat_vel = jnp.pad(velocity, ((0, 0), (0, 1), (0, 1), (0, 0))).reshape(3, -1)
        marker_vel = jnp.zeros((3, SPHERES * MARK), jnp.float32)
        for index, weight in corner_list:
            marker_vel = marker_vel + weight[None] * flat_vel[:, index]
        marker_vel = marker_vel.reshape(3, SPHERES, MARK)
        push = jax.ops.segment_sum((pair_normal * contact_force[None]).T, own_index, SPHERES).T
        sphere_vel = jnp.mean(marker_vel, axis=2) + contact_gain * push
        multiplier = multiplier + rigid_step * (sphere_vel[:, :, None] - marker_vel)
        own_vel = sphere_vel[:, own_index]
        partner_vel = jnp.where(valid[None], sphere_vel[:, partner_index], jnp.float32(0.0))
        closing = jnp.sum(pair_normal * (partner_vel - own_vel), axis=0)
        contact_force = jnp.maximum(jnp.float32(0.0), contact_force - contact_step * (pair_gap + closing))
    return velocity, multiplier, contact_force
```

```python
import functools

import jax
import jax.numpy as jnp
from jax import lax
from jax.experimental import pallas as pl
from jax.experimental.pallas import tpu as pltpu
from jax.sharding import PartitionSpec as P

ITERS = 2
SWEEPS = 2

base_diag = 1.0
spread_gain = 0.25
rigid_step = 0.5
contact_step = 0.5
contact_gain = 0.5

F32 = jnp.float32
BF16 = jnp.bfloat16

LO = SWEEPS
HI = SWEEPS + 1
ROWS = 16
CHUNK = 256


def swaps(along, axes, sizes):
    across = 1 - along
    lists = []
    for kind in (1, 0):
        pairs = []
        for wide in range(sizes[0]):
            for narrow in range(sizes[1]):
                here = [wide, narrow]
                there = list(here)
                spot = here[along]
                there[along] = spot ^ 1 if kind == 0 else ((spot + 1) ^ 1) - 1
                if not 0 <= there[along] < sizes[along]:
                    there = list(here)
                    there[across] = here[across] ^ 1
                    if there[across] >= sizes[across]:
                        continue
                pairs.append((here[0] * sizes[1] + here[1], there[0] * sizes[1] + there[1]))
        lists.append((kind, pairs))
    return lists


def swap(first, second, along):
    axes = ("wide", "narrow")
    sizes = (lax.axis_size("wide"), lax.axis_size("narrow"))
    got = {}
    for kind, pairs in swaps(along, axes, sizes):
        got[kind] = lax.ppermute(first if kind == 0 else second, axes, pairs)
    return got[0], got[1]


class Side:
    def __init__(self, axis):
        self.spot = lax.axis_index(axis)
        self.even = lax.rem(self.spot, 2) == 0
        self.has_down = self.spot > 0
        self.has_up = self.spot < lax.axis_size(axis) - 1

    def emit(self, write, first, second):
        @pl.when(self.even)
        def _():
            write(first, second)

        @pl.when(jnp.logical_not(self.even))
        def _():
            write(second, first)

    def down(self, first, second, block):
        got = jnp.where(self.even, second[block], first[block])
        return jnp.where(self.has_down, got, F32(0.0))

    def up(self, first, second, block):
        got = jnp.where(self.even, first[block], second[block])
        return jnp.where(self.has_up, got, F32(0.0))


def zrow(x, y):
    return ROWS * (x + LO + 1) + y + LO


def geometry(cell_ref, frac_ref, s, start, span, dims):
    bx, by, depth = dims
    at = pl.ds(start, span)
    cell = cell_ref[pl.ds(s, 1), at]
    z_bits, y_bits = depth.bit_length() - 1, by.bit_length() - 1
    cz = cell & (depth - 1)
    cy = (cell >> z_bits) & (by - 1)
    cx = cell >> (z_bits + y_bits)
    px = cx.astype(F32) + frac_ref[0, pl.ds(s, 1), at]
    py = cy.astype(F32) + frac_ref[1, pl.ds(s, 1), at]
    pz = cz.astype(F32) + frac_ref[2, pl.ds(s, 1), at]
    ids = lax.broadcasted_iota(jnp.int32, (16, span), 0).astype(F32)
    wx = jnp.maximum(F32(0.0), 1.0 - jnp.abs(ids - px))
    wy = jnp.maximum(F32(0.0), 1.0 - jnp.abs(ids - py))
    plane = [wx[x : x + 1] * wy[0:by] for x in range(bx + 1)]
    plane.append(wx * wy[by : by + 1])
    plane = jnp.concatenate(plane, axis=0)
    ids = lax.broadcasted_iota(jnp.int32, (depth, span), 0).astype(F32)
    deep = jnp.maximum(F32(0.0), 1.0 - jnp.abs(ids - pz))
    high = deep.astype(BF16)
    low = (deep - high.astype(F32)).astype(BF16)
    return plane, jnp.concatenate([high, low], axis=0)


def chunks(body, spheres, markers):
    span = min(CHUNK, markers)
    for s in range(spheres):

        def step(i, carry, s=s):
            body(s, pl.multiple_of(i * span, span), span)
            return carry

        lax.fori_loop(0, markers // span, step, 0)


def spread(mult_ref, cell_ref, frac_ref, force_ref, total, out_ref, dims):
    bx, by, depth = dims
    comps, spheres, markers = mult_ref.shape
    count = (bx + 1) * by + 16
    total[...] = jnp.zeros_like(total)

    def body(s, start, span):
        plane, deep = geometry(cell_ref, frac_ref, s, start, span, dims)
        rows = [
            plane * (spread_gain * mult_ref[c, pl.ds(s, 1), pl.ds(start, span)])
            for c in range(comps)
        ]
        rest = total.shape[0] - comps * count
        if rest:
            rows.append(jnp.zeros((rest, span), F32))
        rows = jnp.concatenate(rows, axis=0)
        high = rows.astype(BF16)
        low = (rows - high.astype(F32)).astype(BF16)
        dims_nt = (((1,), (1,)), ((), ()))
        total[...] += lax.dot_general(
            high, deep, dims_nt, preferred_element_type=F32
        ) + lax.dot_general(low, deep, dims_nt, preferred_element_type=F32)

    chunks(body, spheres, markers)
    own = bx * by
    for c in range(comps):
        part = total[c * count : (c + 1) * count, :]
        part = part[:, :depth] + part[:, depth:]
        out_ref[c, :own, :] = part[:own] + force_ref[c]
        out_ref[c, own:, :] = part[own:]


def sample(vel, cell_ref, frac_ref, stack, mv, dims):
    bx, by, depth = dims
    comps, spheres, markers = mv.shape
    count = (bx + 1) * by + 16
    stack[...] = jnp.zeros_like(stack)
    for c in range(comps):
        for x in range(bx + 1):
            at = zrow(x, 0)
            stack[c * count + x * by : c * count + (x + 1) * by, :] = vel[c, at : at + by, :]
            at = zrow(x, by)
            stack[c * count + (bx + 1) * by + x : c * count + (bx + 1) * by + x + 1, :] = vel[
                c, at : at + 1, :
            ]
    whole = stack[...]
    high = whole.astype(BF16)
    low = (whole - high.astype(F32)).astype(BF16)
    high = jnp.concatenate([high, high], axis=1)
    low = jnp.concatenate([low, low], axis=1)

    def body(s, start, span):
        plane, deep = geometry(cell_ref, frac_ref, s, start, span, dims)
        near = jnp.dot(high, deep, preferred_element_type=F32) + jnp.dot(
            low, deep, preferred_element_type=F32
        )
        for c in range(comps):
            mv[c, pl.ds(s, 1), pl.ds(start, span)] = jnp.sum(
                near[c * count : (c + 1) * count] * plane, axis=0, keepdims=True
            )

    chunks(body, spheres, markers)


def narrow_payload(up, down, vel, mu, rhs, sv, dims):
    bx, by, _ = dims
    comps = vel.shape[0]
    v_blocks, r_blocks = comps * HI, comps * 2

    def strip(ref, y):
        return ref[pl.ds(y, bx, stride=by), :]

    for c in range(comps):
        for i in range(LO):
            up[c * HI + i] = strip(vel.at[c], by - LO + i)
        for i in range(LO, HI):
            up[c * HI + i] = jnp.zeros((bx, vel.shape[2]), F32)
        for i in range(HI):
            down[c * HI + i] = strip(vel.at[c], i)
        up[v_blocks + 2 * c] = strip(rhs.at[c], by - 1)
        tail = (bx + 1) * by
        up[v_blocks + 2 * c + 1] = rhs[c, tail : tail + bx, :]
        for i in range(2):
            down[v_blocks + 2 * c + i] = strip(rhs.at[c], i)
        far = bx * by
        edge = v_blocks + r_blocks
        up[edge, 2 * c : 2 * c + 1, :] = rhs[c, far + by - 1 : far + by, :]
        up[edge, 2 * c + 1 : 2 * c + 2, :] = rhs[c, tail + bx : tail + bx + 1, :]
        down[edge, 2 * c : 2 * c + 2, :] = rhs[c, far : far + 2, :]
    edge = v_blocks + r_blocks
    for part in (up, down):
        part[edge, 2 * comps :, :] = jnp.zeros((8 - 2 * comps, vel.shape[2]), F32)
        if sv is not None:
            part[edge + 1] = sv
    if mu is not None:
        for i in range(LO):
            up[edge + 1 + i] = strip(mu, by - LO + i)
        for i in range(LO, HI):
            up[edge + 1 + i] = jnp.zeros((bx, vel.shape[2]), F32)
        for i in range(HI):
            down[edge + 1 + i] = strip(mu, i)


def first_kernel(dims, vel, force, vclass, table, mult, cell, frac, first, second, rhs, mu, total):
    value = jnp.zeros(vclass.shape, F32)
    for k in range(table.shape[0]):
        value = value + jnp.where(vclass[...] == k, table[k], F32(0.0))
    mu[...] = value
    spread(mult, cell, frac, force, total, rhs, dims)
    side = Side("narrow")
    side.emit(
        lambda up, down: narrow_payload(up, down, vel, mu, rhs, None, dims), first, second
    )


def pack_kernel(dims, has_mu, got_a, got_b, vel, rhs, extra, first, second):
    bx, by, depth = dims
    comps = vel.shape[0]
    narrow, wide = Side("narrow"), Side("wide")
    v_blocks, r_blocks = comps * HI, comps * 2
    edge = v_blocks + r_blocks
    down_of = functools.partial(narrow.down, got_a, got_b)
    up_of = functools.partial(narrow.up, got_a, got_b)
    low = {}
    high = {}
    for k in list(range(v_blocks)) + ([edge + 1 + i for i in range(HI)] if has_mu else []):
        low[k], high[k] = down_of(k), up_of(k)
    for k in range(v_blocks, edge + 1):
        low[k], high[k] = down_of(k), up_of(k)

    def field_plane(out, k, own, base, x):
        out[k] = jnp.zeros((ROWS, depth), F32)
        for i in range(LO):
            out[k, i : i + 1, :] = low[base + i][x : x + 1]
        out[k, LO : LO + by, :] = own[x * by : (x + 1) * by, :]
        for i in range(HI):
            out[k, LO + by + i : LO + by + i + 1, :] = high[base + i][x : x + 1]

    def rhs_plane(out, k, c, x):
        def row(table, i):
            if x == bx:
                return table[edge][2 * c + i : 2 * c + i + 1]
            return table[v_blocks + 2 * c + i][x : x + 1]

        tail = (bx + 1) * by + x
        out[k] = jnp.zeros((ROWS, depth), F32)
        out[k, LO - 1 : LO, :] = row(low, 0)
        out[k, LO : LO + by, :] = rhs[c, x * by : (x + 1) * by, :]
        out[k, LO : LO + 1, :] += row(low, 1)
        out[k, LO + by : LO + by + 1, :] = rhs[c, tail : tail + 1, :] + row(high, 0)
        out[k, LO + by + 1 : LO + by + 2, :] = row(high, 1)

    def write(up, down):
        for c in range(comps):
            for i in range(LO):
                field_plane(up, c * HI + i, vel.at[c], c * HI, bx - LO + i)
            for i in range(LO, HI):
                up[c * HI + i] = jnp.zeros((ROWS, depth), F32)
            for i in range(HI):
                field_plane(down, c * HI + i, vel.at[c], c * HI, i)
            for i in range(2):
                rhs_plane(up, v_blocks + 2 * c + i, c, bx - 1 + i)
                rhs_plane(down, v_blocks + 2 * c + i, c, i)
        if has_mu:
            for i in range(LO):
                field_plane(up, edge + i, extra, edge + 1, bx - LO + i)
            for i in range(LO, HI):
                up[edge + i] = jnp.zeros((ROWS, depth), F32)
            for i in range(HI):
                field_plane(down, edge + i, extra, edge + 1, i)
        else:
            for part in (up, down):
                part[edge, 0:8, :] = down_of(edge + 1)
                part[edge, 8:16, :] = extra[...]
                part[edge + 1, 0:8, :] = up_of(edge + 1)
                part[edge + 1, 8:16, :] = jnp.zeros((8, depth), F32)

    wide.emit(write, first, second)


def assemble(dims, vel, mu, rhs, near, far, narrow, wide, ext):
    bx, by, depth = dims
    comps = vel.shape[0]
    v_blocks, r_blocks = comps * HI, comps * 2
    edge = v_blocks + r_blocks
    low = functools.partial(narrow.down, *near)
    high = functools.partial(narrow.up, *near)
    left = functools.partial(wide.down, *far)
    right = functools.partial(wide.up, *far)

    def column(y):
        return pl.ds(zrow(0, y), bx, stride=ROWS)

    def plane(x):
        return pl.ds(zrow(x, -LO), ROWS)

    def field(f, own, base, far_base):
        ext[f] = jnp.zeros(ext.shape[1:], F32)
        for x in range(bx):
            ext[f, zrow(x, 0) : zrow(x, by), :] = own[x * by : (x + 1) * by, :]
        for i in range(LO):
            ext[f, column(i - LO), :] = low(base + i)
            ext[f, plane(i - LO), :] = left(far_base + i)
        for i in range(HI):
            ext[f, column(by + i), :] = high(base + i)
            ext[f, plane(bx + i), :] = right(far_base + i)

    for c in range(comps):
        field(c, vel.at[c], c * HI, c * HI)
    if mu is not None:
        field(2 * comps, mu, edge + 1, edge)
    low_edge, high_edge = low(edge), high(edge)
    for c in range(comps):
        f = comps + c
        ext[f] = jnp.zeros(ext.shape[1:], F32)
        for x in range(bx + 1):
            ext[f, zrow(x, 0) : zrow(x, by), :] = rhs[c, x * by : (x + 1) * by, :]
        tail = (bx + 1) * by
        b = v_blocks + 2 * c
        ext[f, column(-1), :] = low(b)
        ext[f, column(0), :] += low(b + 1)
        ext[f, column(by), :] = rhs[c, tail : tail + bx, :] + high(b)
        ext[f, column(by + 1), :] = high(b + 1)
        for y, got in (
            (-1, low_edge[2 * c : 2 * c + 1]),
            (0, rhs[c, bx * by : bx * by + 1, :] + low_edge[2 * c + 1 : 2 * c + 2]),
            (by, rhs[c, tail + bx : tail + bx + 1, :] + high_edge[2 * c : 2 * c + 1]),
            (by + 1, high_edge[2 * c + 1 : 2 * c + 2]),
        ):
            ext[f, zrow(bx, y) : zrow(bx, y) + 1, :] = got
        ext[f, plane(-1), :] = left(b)
        ext[f, plane(0), :] += left(b + 1)
        ext[f, plane(bx), :] += right(b)
        ext[f, plane(bx + 1), :] = right(b + 1)


def sweeps(dims, comps, mu, narrow, wide, ext, mid, coef):
    bx, by, depth = dims
    shape = (ROWS, depth)
    lane = lax.broadcasted_iota(jnp.int32, shape, 1)
    row = lax.broadcasted_iota(jnp.int32, shape, 0) - LO
    inside_y = jnp.logical_and(
        jnp.logical_or(row >= 0, narrow.has_down), jnp.logical_or(row < by, narrow.has_up)
    )
    first, last = lane == 0, lane == depth - 1

    def at(x, shift=0):
        return pl.ds(zrow(x, -LO) + shift, ROWS)

    for x in range(-LO + 1, bx + HI - 1):
        here = mu[at(x), :]
        down_x = 0.5 * (here + mu[at(x - 1), :])
        up_x = 0.5 * (here + mu[at(x + 1), :])
        down_y = 0.5 * (here + mu[at(x, -1), :])
        up_y = 0.5 * (here + mu[at(x, 1), :])
        down_z = 0.5 * (here + jnp.where(first, 0.0, pltpu.roll(here, 1, 1)))
        up_z = 0.5 * (here + jnp.where(last, 0.0, pltpu.roll(here, depth - 1, 1)))
        diagonal = base_diag + down_x + up_x + down_y + up_y + down_z + up_z
        inside = inside_y
        if x < 0:
            inside = jnp.logical_and(inside, wide.has_down)
        if x >= bx:
            inside = jnp.logical_and(inside, wide.has_up)
        coef[0, at(x), :] = down_x
        coef[1, at(x), :] = down_y
        coef[2, at(x), :] = up_y
        coef[3, at(x), :] = jnp.where(first, 0.0, down_z)
        coef[4, at(x), :] = jnp.where(last, 0.0, up_z)
        coef[5, at(x), :] = jnp.where(inside, 1.0 / diagonal, 0.0)
        if x == bx + HI - 2:
            coef[0, at(x + 1), :] = up_x

    for source, target, span in (
        (ext, mid, range(-1, bx + 2)),
        (mid, ext, range(0, bx + 1)),
    ):
        for x in span:
            down_x, up_x = coef[0, at(x), :], coef[0, at(x + 1), :]
            down_y, up_y = coef[1, at(x), :], coef[2, at(x), :]
            down_z, up_z, inverse = coef[3, at(x), :], coef[4, at(x), :], coef[5, at(x), :]
            for c in range(comps):
                here = source[c, at(x), :]
                value = (
                    ext[comps + c, at(x), :]
                    + down_x * source[c, at(x - 1), :]
                    + up_x * source[c, at(x + 1), :]
                    + down_y * source[c, at(x, -1), :]
                    + up_y * source[c, at(x, 1), :]
                    + down_z * pltpu.roll(here, 1, 1)
                    + up_z * pltpu.roll(here, depth - 1, 1)
                )
                target[c, at(x), :] = value * inverse


def move_markers(mult, mv, sphere, normal, contact, new_mult, sv):
    comps, spheres, markers = mult.shape
    sv[...] = jnp.zeros_like(sv)
    for c in range(comps):
        load = normal[c : c + 1, :] * contact
        mean = jnp.sum(mv[c], axis=1, keepdims=True) / markers
        for s in range(spheres):
            push = jnp.sum(jnp.where(sphere == s, load, 0.0), axis=1, keepdims=True)
            speed = mean[s : s + 1] + contact_gain * push
            sv[s * comps + c : s * comps + c + 1, :] = jnp.broadcast_to(speed, (1, sv.shape[1]))
            new_mult[c, s : s + 1, :] = mult[c, s : s + 1, :] + rigid_step * (
                speed - mv[c, s : s + 1, :]
            )


def new_contact(blocks, sphere, partner, normal, gap, contact, comps, spheres):
    pairs = contact.shape[1]
    closing = jnp.zeros_like(contact)
    for c in range(comps):
        speed = jnp.zeros_like(contact)
        for q, block in enumerate(blocks):
            for s in range(spheres):
                line = block[s * comps + c : s * comps + c + 1, :pairs]
                speed = speed + jnp.where(partner == q * spheres + s, line, 0.0)
        own = jnp.zeros_like(contact)
        for s in range(spheres):
            line = blocks[4][s * comps + c : s * comps + c + 1, :pairs]
            own = own + jnp.where(sphere == s, line, 0.0)
        closing = closing + normal[c : c + 1, :] * (speed - own)
    return jnp.maximum(0.0, contact - contact_step * (gap + closing))


def middle_kernel(
    dims,
    near_a, near_b, far_a, far_b,
    vel, mu, rhs, force, mult, cell, frac, sphere, normal, contact,
    first, second, vel_out, rhs_out, mu_out, mult_out, sv,
    ext, mid, coef, stack, mv, total,
):
    bx, by, _ = dims
    comps = vel.shape[0]
    narrow, wide = Side("narrow"), Side("wide")
    assemble(dims, vel, mu, rhs, (near_a, near_b), (far_a, far_b), narrow, wide, ext)
    mu_out[...] = ext[2 * comps]
    sweeps(dims, comps, ext.at[2 * comps], narrow, wide, ext, mid, coef)
    for c in range(comps):
        for x in range(bx):
            vel_out[c, x * by : (x + 1) * by, :] = ext[c, zrow(x, 0) : zrow(x, by), :]
    sample(ext, cell, frac, stack, mv, dims)
    move_markers(mult, mv, sphere[...], normal, contact[...], mult_out, sv)
    spread(mult_out, cell, frac, force, total, rhs_out, dims)
    narrow.emit(
        lambda up, down: narrow_payload(up, down, vel_out, None, rhs_out, sv[...], dims),
        first,
        second,
    )


def last_kernel(
    dims,
    near_a, near_b, far_a, far_b, old_sv,
    vel, mu, rhs, mult, cell, frac, sphere, partner, normal, gap, contact,
    vel_out, mult_out, contact_out, sv,
    ext, mid, coef, stack, mv,
):
    bx, by, _ = dims
    comps, spheres, _ = mult.shape
    narrow, wide = Side("narrow"), Side("wide")
    assemble(dims, vel, None, rhs, (near_a, near_b), (far_a, far_b), narrow, wide, ext)
    sweeps(dims, comps, mu, narrow, wide, ext, mid, coef)
    for c in range(comps):
        for x in range(bx):
            vel_out[c, x * by : (x + 1) * by, :] = ext[c, zrow(x, 0) : zrow(x, by), :]
    sample(ext, cell, frac, stack, mv, dims)
    edge = comps * HI + comps * 2
    blocks = []
    for get in (wide.down, wide.up):
        both, one = get(far_a, far_b, edge), get(far_a, far_b, edge + 1)
        blocks.append([both[0:8], both[8:16], one[0:8]])
    blocks.insert(
        1,
        [narrow.down(near_a, near_b, edge + 1), old_sv[...], narrow.up(near_a, near_b, edge + 1)],
    )
    now = new_contact(
        sum(blocks, []), sphere[...], partner[...], normal, gap[...], contact[...], comps, spheres
    )
    contact_out[...] = now
    move_markers(mult, mv, sphere[...], normal, now, mult_out, sv)


def gather_kernel(got_a, got_b, sv, out):
    narrow = Side("narrow")
    every = slice(None)
    out[0:8, :] = narrow.down(got_a, got_b, every)
    out[8:16, :] = sv[...]
    out[16:24, :] = narrow.up(got_a, got_b, every)


def contact_kernel(comps, spheres, own, got_a, got_b, sphere, partner, normal, gap, contact, out):
    wide = Side("wide")
    every = slice(None)
    blocks = []
    for part in (wide.down(got_a, got_b, every), own[...], wide.up(got_a, got_b, every)):
        blocks += [part[0:8], part[8:16], part[16:24]]
    out[...] = new_contact(
        blocks, sphere[...], partner[...], normal, gap[...], contact[...], comps, spheres
    )


def call(kernel, name, ins, outs, scratch=(), smem=()):
    vmem = pl.BlockSpec(memory_space=pltpu.VMEM)
    return pl.pallas_call(
        kernel,
        name=name,
        in_specs=[
            pl.BlockSpec(memory_space=pltpu.SMEM) if i in smem else vmem for i in range(len(ins))
        ],
        out_specs=[vmem] * len(outs),
        out_shape=[jax.ShapeDtypeStruct(shape, F32) for shape in outs],
        scratch_shapes=[pltpu.VMEM(shape, F32) for shape in scratch],
    )(*ins)


def local(
    velocity,
    force,
    visc_class,
    visc_table,
    multiplier,
    marker_cell,
    marker_frac,
    pair_sphere,
    pair_partner,
    pair_normal,
    pair_gap,
    contact_force,
):
    comps, bx, by, depth = velocity.shape
    spheres, markers = marker_cell.shape
    pairs = pair_sphere.shape[0]
    dims = (bx, by, depth)
    own = bx * by
    count = (bx + 1) * by + 16
    padded = -(-comps * count // 16) * 16
    long = ROWS * (bx + LO + HI + 2)
    edge = comps * HI + comps * 2
    vel = velocity.reshape(comps, own, depth)
    force = force.reshape(comps, own, depth)
    vclass = visc_class.reshape(own, depth)
    sphere = pair_sphere.reshape(1, pairs)
    partner = pair_partner.reshape(1, pairs)
    gap = pair_gap.reshape(1, pairs)
    contact = contact_force.reshape(1, pairs)

    total = (padded, 2 * depth)
    ext = (2 * comps, long, depth)
    ext_mu = (2 * comps + 1, long, depth)
    mid = (comps, long, depth)
    coef = (6, long, depth)
    stack = (padded, depth)
    marks = (comps, spheres, markers)
    rows = (comps, count, depth)
    field = (comps, own, depth)
    strips = (edge + 1 + HI, bx, depth)
    planes = (edge + HI, ROWS, depth)

    first, second, rhs, mu = call(
        functools.partial(first_kernel, dims),
        "spread_first",
        [vel, force, vclass, visc_table, multiplier, marker_cell, marker_frac],
        [strips, strips, rows, (own, depth)],
        [total],
        smem=(3,),
    )
    near = swap(first, second, 1)
    first, second = call(
        functools.partial(pack_kernel, dims, True),
        "pack_first",
        [*near, vel, rhs, mu],
        [planes, planes],
    )
    far = swap(first, second, 0)
    strips = (edge + 2, bx, depth)
    planes = (edge + 2, ROWS, depth)
    first, second, vel, rhs, mu, multiplier, sv = call(
        functools.partial(middle_kernel, dims),
        "iterate",
        [*near, *far, vel, mu, rhs, force, multiplier, marker_cell, marker_frac]
        + [sphere, pair_normal, contact],
        [strips, strips, field, rows, (long, depth), marks, (8, depth)],
        [ext_mu, mid, coef, stack, marks, total],
    )
    near = swap(first, second, 1)
    first, second = call(
        functools.partial(pack_kernel, dims, False),
        "pack_second",
        [*near, vel, rhs, sv],
        [planes, planes],
    )
    far = swap(first, second, 0)
    vel, multiplier, contact, sv = call(
        functools.partial(last_kernel, dims),
        "finish",
        [*near, *far, sv, vel, mu, rhs, multiplier, marker_cell, marker_frac]
        + [sphere, partner, pair_normal, gap, contact],
        [field, marks, (1, pairs), (8, depth)],
        [ext, mid, coef, stack, marks],
    )
    near = swap(sv, sv, 1)
    (three,) = call(gather_kernel, "gather", [*near, sv], [(24, depth)])
    far = swap(three, three, 0)
    (contact,) = call(
        functools.partial(contact_kernel, comps, spheres),
        "contact",
        [three, *far, sphere, partner, pair_normal, gap, contact],
        [(1, pairs)],
    )
    return (vel.reshape(comps, bx, by, depth), multiplier, contact.reshape(pairs))


def solution(mesh):
    in_specs = (
        P(None, "wide", "narrow", None),
        P(None, "wide", "narrow", None),
        P("wide", "narrow", None),
        P(),
        P(None, ("wide", "narrow"), None),
        P(("wide", "narrow"), None),
        P(None, ("wide", "narrow"), None),
        P(("wide", "narrow")),
        P(("wide", "narrow")),
        P(None, ("wide", "narrow")),
        P(("wide", "narrow")),
        P(("wide", "narrow")),
    )
    out_specs = (
        P(None, "wide", "narrow", None),
        P(None, ("wide", "narrow"), None),
        P(("wide", "narrow")),
    )
    return jax.shard_map(local, mesh=mesh, in_specs=in_specs, out_specs=out_specs, check_vma=False)
```

```python
import functools

import jax
import jax.numpy as jnp
from jax import lax
from jax.experimental import pallas as pl
from jax.experimental.pallas import tpu as pltpu
from jax.sharding import PartitionSpec as P

ITERS = 2
SWEEPS = 2

base_diag = 1.0
spread_gain = 0.25
rigid_step = 0.5
contact_step = 0.5
contact_gain = 0.5

F32 = jnp.float32
BF16 = jnp.bfloat16

LO = SWEEPS
HI = SWEEPS + 1
ROWS = 16
CHUNK = 512
GRANT = 16 * 1024 * 1024


def swaps(along, axes, sizes):
    across = 1 - along
    lists = []
    for kind in (1, 0):
        pairs = []
        for wide in range(sizes[0]):
            for narrow in range(sizes[1]):
                here = [wide, narrow]
                there = list(here)
                spot = here[along]
                there[along] = spot ^ 1 if kind == 0 else ((spot + 1) ^ 1) - 1
                if not 0 <= there[along] < sizes[along]:
                    there = list(here)
                    there[across] = here[across] ^ 1
                    if there[across] >= sizes[across]:
                        continue
                pairs.append((here[0] * sizes[1] + here[1], there[0] * sizes[1] + there[1]))
        lists.append((kind, pairs))
    return lists


def swap(first, second, along):
    axes = ("wide", "narrow")
    sizes = (lax.axis_size("wide"), lax.axis_size("narrow"))
    got = {}
    for kind, pairs in swaps(along, axes, sizes):
        got[kind] = lax.ppermute(first if kind == 0 else second, axes, pairs)
    return got[0], got[1]


class Side:
    def __init__(self, axis):
        self.spot = lax.axis_index(axis)
        self.even = lax.rem(self.spot, 2) == 0
        self.has_down = self.spot > 0
        self.has_up = self.spot < lax.axis_size(axis) - 1

    def emit(self, write, first, second):
        @pl.when(self.even)
        def _():
            write(first, second)

        @pl.when(jnp.logical_not(self.even))
        def _():
            write(second, first)

    def down(self, first, second, block):
        got = jnp.where(self.even, second[block], first[block])
        return jnp.where(self.has_down, got, F32(0.0))

    def up(self, first, second, block):
        got = jnp.where(self.even, first[block], second[block])
        return jnp.where(self.has_up, got, F32(0.0))


def zrow(x, y):
    return ROWS * (x + LO + 1) + y + LO


def hat(position, count):
    ids = lax.broadcasted_iota(jnp.int32, (count, position.shape[1]), 0).astype(F32)
    return jnp.maximum(F32(0.0), 1.0 - jnp.abs(ids - position))


def parts(value):
    high = value.astype(BF16)
    return high, (value - high.astype(F32)).astype(BF16)


def geometry(cell_ref, frac_ref, s, start, span, plane, deep, dims):
    bx, by, depth = dims
    markers = cell_ref.shape[1]
    at = pl.ds(start, span)
    to = pl.ds(s * markers + start, span)
    cell = cell_ref[s : s + 1, at]
    z_bits, y_bits = depth.bit_length() - 1, by.bit_length() - 1
    cz = cell & (depth - 1)
    cy = (cell >> z_bits) & (by - 1)
    cx = cell >> (z_bits + y_bits)
    wx = hat(cx.astype(F32) + frac_ref[0, s : s + 1, at], 16)
    wy = hat(cy.astype(F32) + frac_ref[1, s : s + 1, at], 16)
    for x in range(bx + 1):
        plane[x * by : (x + 1) * by, to] = wx[x : x + 1] * wy[0:by]
    plane[(bx + 1) * by :, to] = wx * wy[by : by + 1]
    high, low = parts(hat(cz.astype(F32) + frac_ref[2, s : s + 1, at], depth))
    deep[0:depth, to] = high
    deep[depth : 2 * depth, to] = low


def chunks(spheres, markers):
    span = min(CHUNK, markers)
    return [(s, start, span) for s in range(spheres) for start in range(0, markers, span)]


def weighted(rows, deep):
    high, low = parts(rows)
    both = lax.dot_general(
        jnp.concatenate([high, low], axis=1),
        jnp.concatenate([deep, deep], axis=1),
        (((1,), (1,)), ((), ())),
        preferred_element_type=F32,
    )
    half = both.shape[1] // 2
    return both[:, :half] + both[:, half:]


def spread(mult_ref, plane, deep, force_ref, total, out_ref, dims, prepare=None):
    bx, by, depth = dims
    comps, spheres, markers = mult_ref.shape
    count = plane.shape[0]
    for k, (s, start, span) in enumerate(chunks(spheres, markers)):
        if prepare is not None:
            prepare(s, start, span)
        at = pl.ds(s * markers + start, span)
        weights = plane[:, at]
        rows = [
            weights * (spread_gain * mult_ref[c, s : s + 1, pl.ds(start, span)])
            for c in range(comps)
        ]
        rest = total.shape[0] - comps * count
        if rest:
            rows.append(jnp.zeros((rest, span), F32))
        add = weighted(jnp.concatenate(rows, axis=0), deep[:, at])
        if k:
            total[...] += add
        else:
            total[...] = add
    own = bx * by
    for c in range(comps):
        part = total[c * count : (c + 1) * count, :]
        out_ref[c, :own, :] = part[:own] + force_ref[c]
        out_ref[c, own:, :] = part[own:]


def stack_up(vel, stack, count, dims):
    bx, by, _ = dims
    comps = stack.shape[0] // count
    stack[...] = jnp.zeros_like(stack)
    for c in range(comps):
        for x in range(bx + 1):
            at = zrow(x, 0)
            stack[c * count + x * by : c * count + (x + 1) * by, :] = vel[c, at : at + by, :]
            at = zrow(x, by)
            stack[c * count + (bx + 1) * by + x : c * count + (bx + 1) * by + x + 1, :] = vel[
                c, at : at + 1, :
            ]


def sample(stack, plane, deep, mv):
    comps, spheres, markers = mv.shape
    count = plane.shape[0]
    high, low = parts(stack[...])
    lhs = jnp.concatenate([high, high, low, low], axis=1)
    for s, start, span in chunks(spheres, markers):
        at = pl.ds(s * markers + start, span)
        weights = deep[:, at]
        near = jnp.dot(
            lhs, jnp.concatenate([weights, weights], axis=0), preferred_element_type=F32
        )
        for c in range(comps):
            mv[c, s : s + 1, pl.ds(start, span)] = jnp.sum(
                near[c * count : (c + 1) * count] * plane[:, at], axis=0, keepdims=True
            )


def narrow_payload(up, down, vel, mu, rhs, sv, dims):
    bx, by, _ = dims
    comps = vel.shape[0]
    v_blocks, r_blocks = comps * HI, comps * 2

    def strip(ref, y):
        return ref[pl.ds(y, bx, stride=by), :]

    for c in range(comps):
        for i in range(LO):
            up[c * HI + i] = strip(vel.at[c], by - LO + i)
        for i in range(LO, HI):
            up[c * HI + i] = jnp.zeros((bx, vel.shape[2]), F32)
        for i in range(HI):
            down[c * HI + i] = strip(vel.at[c], i)
        up[v_blocks + 2 * c] = strip(rhs.at[c], by - 1)
        tail = (bx + 1) * by
        up[v_blocks + 2 * c + 1] = rhs[c, tail : tail + bx, :]
        for i in range(2):
            down[v_blocks + 2 * c + i] = strip(rhs.at[c], i)
        far = bx * by
        edge = v_blocks + r_blocks
        up[edge, 2 * c : 2 * c + 1, :] = rhs[c, far + by - 1 : far + by, :]
        up[edge, 2 * c + 1 : 2 * c + 2, :] = rhs[c, tail + bx : tail + bx + 1, :]
        down[edge, 2 * c : 2 * c + 2, :] = rhs[c, far : far + 2, :]
    edge = v_blocks + r_blocks
    for part in (up, down):
        part[edge, 2 * comps :, :] = jnp.zeros((8 - 2 * comps, vel.shape[2]), F32)
        if sv is not None:
            part[edge + 1] = sv
    if mu is not None:
        for i in range(LO):
            up[edge + 1 + i] = strip(mu, by - LO + i)
        for i in range(LO, HI):
            up[edge + 1 + i] = jnp.zeros((bx, vel.shape[2]), F32)
        for i in range(HI):
            down[edge + 1 + i] = strip(mu, i)


def first_kernel(dims, count, *refs):
    ins, outs, scratch = refs[:12], refs[12:26], refs[26:]
    vel, force, vclass, table, mult, cell, frac = ins[:7]
    first, second, rhs, mu, plane, deep, vel_out, force_out, mult_out = outs[:9]
    class_here, table_here, cell_here, frac_here, total, sems = scratch
    copies = [
        pltpu.make_async_copy(source, target, sems.at[i])
        for i, (source, target) in enumerate(
            [
                (cell, cell_here),
                (frac, frac_here),
                (mult, mult_out),
                (force, force_out),
                (table, table_here),
                (vclass, class_here),
                (vel, vel_out),
            ]
            + list(zip(ins[7:], outs[9:]))
        )
    ]
    for copy in copies:
        copy.start()
    for copy in copies[:4]:
        copy.wait()

    def prepare(s, start, span):
        geometry(cell_here, frac_here, s, start, span, plane, deep, dims)

    spread(mult_out, plane, deep, force_out, total, rhs, dims, prepare)
    for copy in copies[4:]:
        copy.wait()
    value = jnp.zeros(class_here.shape, F32)
    for k in range(table.shape[0]):
        value = value + jnp.where(class_here[...] == k, table_here[k], F32(0.0))
    mu[...] = value
    side = Side("narrow")
    side.emit(
        lambda up, down: narrow_payload(up, down, vel_out, mu, rhs, None, dims), first, second
    )


def mean_kernel(plane, deep, out):
    spheres, count, _ = out.shape
    markers = plane.shape[1] // spheres
    for s in range(spheres):
        at = pl.ds(s * markers, markers)
        rows = plane[:, at]
        rest = -count % 16
        if rest:
            rows = jnp.concatenate([rows, jnp.zeros((rest, markers), F32)], axis=0)
        out[s] = weighted(rows, deep[:, at])[:count] * (1.0 / markers)


def pack_kernel(dims, has_mu, got_a, got_b, vel, rhs, extra, first, second):
    bx, by, depth = dims
    comps = vel.shape[0]
    narrow, wide = Side("narrow"), Side("wide")
    v_blocks, r_blocks = comps * HI, comps * 2
    edge = v_blocks + r_blocks
    down_of = functools.partial(narrow.down, got_a, got_b)
    up_of = functools.partial(narrow.up, got_a, got_b)
    low = {}
    high = {}
    for k in list(range(v_blocks)) + ([edge + 1 + i for i in range(HI)] if has_mu else []):
        low[k], high[k] = down_of(k), up_of(k)
    for k in range(v_blocks, edge + 1):
        low[k], high[k] = down_of(k), up_of(k)

    def field_plane(out, k, own, base, x):
        out[k] = jnp.zeros((ROWS, depth), F32)
        for i in range(LO):
            out[k, i : i + 1, :] = low[base + i][x : x + 1]
        out[k, LO : LO + by, :] = own[x * by : (x + 1) * by, :]
        for i in range(HI):
            out[k, LO + by + i : LO + by + i + 1, :] = high[base + i][x : x + 1]

    def rhs_plane(out, k, c, x):
        def row(table, i):
            if x == bx:
                return table[edge][2 * c + i : 2 * c + i + 1]
            return table[v_blocks + 2 * c + i][x : x + 1]

        tail = (bx + 1) * by + x
        out[k] = jnp.zeros((ROWS, depth), F32)
        out[k, LO - 1 : LO, :] = row(low, 0)
        out[k, LO : LO + by, :] = rhs[c, x * by : (x + 1) * by, :]
        out[k, LO : LO + 1, :] += row(low, 1)
        out[k, LO + by : LO + by + 1, :] = rhs[c, tail : tail + 1, :] + row(high, 0)
        out[k, LO + by + 1 : LO + by + 2, :] = row(high, 1)

    def write(up, down):
        for c in range(comps):
            for i in range(LO):
                field_plane(up, c * HI + i, vel.at[c], c * HI, bx - LO + i)
            for i in range(LO, HI):
                up[c * HI + i] = jnp.zeros((ROWS, depth), F32)
            for i in range(HI):
                field_plane(down, c * HI + i, vel.at[c], c * HI, i)
            for i in range(2):
                rhs_plane(up, v_blocks + 2 * c + i, c, bx - 1 + i)
                rhs_plane(down, v_blocks + 2 * c + i, c, i)
        if has_mu:
            for i in range(LO):
                field_plane(up, edge + i, extra, edge + 1, bx - LO + i)
            for i in range(LO, HI):
                up[edge + i] = jnp.zeros((ROWS, depth), F32)
            for i in range(HI):
                field_plane(down, edge + i, extra, edge + 1, i)
        else:
            for part in (up, down):
                part[edge, 0:8, :] = down_of(edge + 1)
                part[edge, 8:16, :] = extra[...]
                part[edge + 1, 0:8, :] = up_of(edge + 1)
                part[edge + 1, 8:16, :] = jnp.zeros((8, depth), F32)

    wide.emit(write, first, second)


def assemble(dims, vel, mu, rhs, near, far, narrow, wide, ext):
    bx, by, depth = dims
    comps = vel.shape[0]
    v_blocks, r_blocks = comps * HI, comps * 2
    edge = v_blocks + r_blocks
    low = functools.partial(narrow.down, *near)
    high = functools.partial(narrow.up, *near)
    left = functools.partial(wide.down, *far)
    right = functools.partial(wide.up, *far)

    def column(y):
        return pl.ds(zrow(0, y), bx, stride=ROWS)

    def plane(x):
        return pl.ds(zrow(x, -LO), ROWS)

    def field(f, own, base, far_base):
        ext[f] = jnp.zeros(ext.shape[1:], F32)
        for x in range(bx):
            ext[f, zrow(x, 0) : zrow(x, by), :] = own[x * by : (x + 1) * by, :]
        for i in range(LO):
            ext[f, column(i - LO), :] = low(base + i)
            ext[f, plane(i - LO), :] = left(far_base + i)
        for i in range(HI):
            ext[f, column(by + i), :] = high(base + i)
            ext[f, plane(bx + i), :] = right(far_base + i)

    for c in range(comps):
        field(c, vel.at[c], c * HI, c * HI)
    if mu is not None:
        field(2 * comps, mu, edge + 1, edge)
    low_edge, high_edge = low(edge), high(edge)
    for c in range(comps):
        f = comps + c
        ext[f] = jnp.zeros(ext.shape[1:], F32)
        for x in range(bx + 1):
            ext[f, zrow(x, 0) : zrow(x, by), :] = rhs[c, x * by : (x + 1) * by, :]
        tail = (bx + 1) * by
        b = v_blocks + 2 * c
        ext[f, column(-1), :] = low(b)
        ext[f, column(0), :] += low(b + 1)
        ext[f, column(by), :] = rhs[c, tail : tail + bx, :] + high(b)
        ext[f, column(by + 1), :] = high(b + 1)
        for y, got in (
            (-1, low_edge[2 * c : 2 * c + 1]),
            (0, rhs[c, bx * by : bx * by + 1, :] + low_edge[2 * c + 1 : 2 * c + 2]),
            (by, rhs[c, tail + bx : tail + bx + 1, :] + high_edge[2 * c : 2 * c + 1]),
            (by + 1, high_edge[2 * c + 1 : 2 * c + 2]),
        ):
            ext[f, zrow(bx, y) : zrow(bx, y) + 1, :] = got
        ext[f, plane(-1), :] = left(b)
        ext[f, plane(0), :] += left(b + 1)
        ext[f, plane(bx), :] += right(b)
        ext[f, plane(bx + 1), :] = right(b + 1)


def sweeps(dims, comps, mu, narrow, wide, ext, mid, coef):
    bx, by, depth = dims
    shape = (ROWS, depth)
    lane = lax.broadcasted_iota(jnp.int32, shape, 1)
    row = lax.broadcasted_iota(jnp.int32, shape, 0) - LO
    inside_y = jnp.logical_and(
        jnp.logical_or(row >= 0, narrow.has_down), jnp.logical_or(row < by, narrow.has_up)
    )
    first, last = lane == 0, lane == depth - 1

    def at(x, shift=0):
        return pl.ds(zrow(x, -LO) + shift, ROWS)

    for x in range(-LO + 1, bx + HI - 1):
        here = mu[at(x), :]
        down_x = 0.5 * (here + mu[at(x - 1), :])
        up_x = 0.5 * (here + mu[at(x + 1), :])
        down_y = 0.5 * (here + mu[at(x, -1), :])
        up_y = 0.5 * (here + mu[at(x, 1), :])
        down_z = 0.5 * (here + jnp.where(first, 0.0, pltpu.roll(here, 1, 1)))
        up_z = 0.5 * (here + jnp.where(last, 0.0, pltpu.roll(here, depth - 1, 1)))
        diagonal = base_diag + down_x + up_x + down_y + up_y + down_z + up_z
        inside = inside_y
        if x < 0:
            inside = jnp.logical_and(inside, wide.has_down)
        if x >= bx:
            inside = jnp.logical_and(inside, wide.has_up)
        coef[0, at(x), :] = down_x
        coef[1, at(x), :] = down_y
        coef[2, at(x), :] = up_y
        coef[3, at(x), :] = jnp.where(first, 0.0, down_z)
        coef[4, at(x), :] = jnp.where(last, 0.0, up_z)
        coef[5, at(x), :] = jnp.where(inside, 1.0 / diagonal, 0.0)
        if x == bx + HI - 2:
            coef[0, at(x + 1), :] = up_x

    for source, target, span in (
        (ext, mid, range(-1, bx + 2)),
        (mid, ext, range(0, bx + 1)),
    ):
        for x in span:
            down_x, up_x = coef[0, at(x), :], coef[0, at(x + 1), :]
            down_y, up_y = coef[1, at(x), :], coef[2, at(x), :]
            down_z, up_z, inverse = coef[3, at(x), :], coef[4, at(x), :], coef[5, at(x), :]
            for c in range(comps):
                here = source[c, at(x), :]
                value = (
                    ext[comps + c, at(x), :]
                    + down_x * source[c, at(x - 1), :]
                    + up_x * source[c, at(x + 1), :]
                    + down_y * source[c, at(x, -1), :]
                    + up_y * source[c, at(x, 1), :]
                    + down_z * pltpu.roll(here, 1, 1)
                    + up_z * pltpu.roll(here, depth - 1, 1)
                )
                target[c, at(x), :] = value * inverse


def sphere_pushes(sphere, normal, contact, comps, spheres):
    pushes = {}
    for c in range(comps):
        load = normal[c : c + 1, :] * contact
        for s in range(spheres):
            pushes[c, s] = contact_gain * jnp.sum(
                jnp.where(sphere == s, load, 0.0), axis=1, keepdims=True
            )
    return pushes


def move_markers(mult, mv, sv, new_mult):
    comps, spheres, _ = mult.shape
    for c in range(comps):
        for s in range(spheres):
            row = s * comps + c
            new_mult[c, s : s + 1, :] = mult[c, s : s + 1, :] + rigid_step * (
                sv[row : row + 1, 0:1] - mv[c, s : s + 1, :]
            )


def new_contact(blocks, sphere, partner, normal, gap, contact, comps, spheres):
    pairs = contact.shape[1]
    closing = jnp.zeros_like(contact)
    for c in range(comps):
        speed = jnp.zeros_like(contact)
        for q, block in enumerate(blocks):
            for s in range(spheres):
                line = block[s * comps + c : s * comps + c + 1, :pairs]
                speed = speed + jnp.where(partner == q * spheres + s, line, 0.0)
        own = jnp.zeros_like(contact)
        for s in range(spheres):
            line = blocks[4][s * comps + c : s * comps + c + 1, :pairs]
            own = own + jnp.where(sphere == s, line, 0.0)
        closing = closing + normal[c : c + 1, :] * (speed - own)
    return jnp.maximum(0.0, contact - contact_step * (gap + closing))


def middle_kernel(
    dims,
    near_a, near_b, far_a, far_b,
    vel, mu, rhs, force, mult, plane, deep, sphere, normal, contact,
    first, second, vel_out, rhs_out, mu_out, mult_out, sv,
    ext, mid, coef, stack, mv, total,
):
    bx, by, _ = dims
    comps, spheres, markers = mult.shape
    narrow, wide = Side("narrow"), Side("wide")
    assemble(dims, vel, mu, rhs, (near_a, near_b), (far_a, far_b), narrow, wide, ext)
    mu_out[...] = ext[2 * comps]
    sweeps(dims, comps, ext.at[2 * comps], narrow, wide, ext, mid, coef)
    for c in range(comps):
        for x in range(bx):
            vel_out[c, x * by : (x + 1) * by, :] = ext[c, zrow(x, 0) : zrow(x, by), :]
    stack_up(ext, stack, plane.shape[0], dims)
    sample(stack, plane, deep, mv)
    pushes = sphere_pushes(sphere[...], normal, contact[...], comps, spheres)
    sv[...] = jnp.zeros_like(sv)
    for c in range(comps):
        mean = jnp.sum(mv[c], axis=1, keepdims=True) / markers
        for s in range(spheres):
            row = s * comps + c
            sv[row : row + 1, :] = jnp.broadcast_to(
                mean[s : s + 1] + pushes[c, s], (1, sv.shape[1])
            )
    move_markers(mult, mv, sv, mult_out)
    spread(mult_out, plane, deep, force, total, rhs_out, dims)
    narrow.emit(
        lambda up, down: narrow_payload(up, down, vel_out, None, rhs_out, sv[...], dims),
        first,
        second,
    )


def last_kernel(
    dims,
    near_a, near_b, far_a, far_b, old_sv,
    vel, mu, rhs, means, sphere, partner, normal, gap, contact,
    stack, contact_out, sv,
    ext, mid, coef,
):
    comps = vel.shape[0]
    spheres, count, _ = means.shape
    narrow, wide = Side("narrow"), Side("wide")
    assemble(dims, vel, None, rhs, (near_a, near_b), (far_a, far_b), narrow, wide, ext)
    sweeps(dims, comps, mu, narrow, wide, ext, mid, coef)
    stack_up(ext, stack, count, dims)
    edge = comps * HI + comps * 2
    blocks = []
    for get in (wide.down, wide.up):
        both, one = get(far_a, far_b, edge), get(far_a, far_b, edge + 1)
        blocks.append([both[0:8], both[8:16], one[0:8]])
    blocks.insert(
        1,
        [narrow.down(near_a, near_b, edge + 1), old_sv[...], narrow.up(near_a, near_b, edge + 1)],
    )
    now = new_contact(
        sum(blocks, []), sphere[...], partner[...], normal, gap[...], contact[...], comps, spheres
    )
    contact_out[...] = now
    pushes = sphere_pushes(sphere[...], normal, now, comps, spheres)
    sv[...] = jnp.zeros_like(sv)
    for c in range(comps):
        for s in range(spheres):
            row = s * comps + c
            product = stack[c * count : (c + 1) * count, :] * means[s]
            mean = jnp.sum(jnp.sum(product, axis=0, keepdims=True), axis=1, keepdims=True)
            sv[row : row + 1, :] = jnp.broadcast_to(mean + pushes[c, s], (1, sv.shape[1]))


def marker_kernel(dims, stack, plane, deep, mult, sv, vel_out, mult_out, mv):
    bx, by, _ = dims
    count = plane.shape[0]
    for c in range(mult.shape[0]):
        vel_out[c] = stack[c * count : c * count + bx * by, :]
    sample(stack, plane, deep, mv)
    move_markers(mult, mv, sv, mult_out)


def gather_kernel(got_a, got_b, sv, out):
    narrow = Side("narrow")
    every = slice(None)
    out[0:8, :] = narrow.down(got_a, got_b, every)
    out[8:16, :] = sv[...]
    out[16:24, :] = narrow.up(got_a, got_b, every)


def contact_kernel(comps, spheres, own, got_a, got_b, sphere, partner, normal, gap, contact, out):
    wide = Side("wide")
    every = slice(None)
    blocks = []
    for part in (wide.down(got_a, got_b, every), own[...], wide.up(got_a, got_b, every)):
        blocks += [part[0:8], part[8:16], part[16:24]]
    out[...] = new_contact(
        blocks, sphere[...], partner[...], normal, gap[...], contact[...], comps, spheres
    )


def call(kernel, name, ins, outs, scratch=(), hbm=False):
    vmem = pl.BlockSpec(memory_space=pltpu.VMEM)
    apart = pl.BlockSpec(memory_space=pltpu.HBM)
    outs = [out if isinstance(out, jax.ShapeDtypeStruct) else jax.ShapeDtypeStruct(out, F32) for out in outs]
    if hbm:
        ins = [pltpu.with_memory_space_constraint(x, pltpu.HBM) for x in ins]
    return pl.pallas_call(
        kernel,
        name=name,
        in_specs=[apart if hbm else vmem] * len(ins),
        out_specs=[vmem] * len(outs),
        out_shape=outs,
        scratch_shapes=[
            pltpu.VMEM(shape, F32) if isinstance(shape, tuple) else shape for shape in scratch
        ],
        compiler_params=pltpu.CompilerParams(vmem_limit_bytes=GRANT),
    )(*ins)


def local(
    velocity,
    force,
    visc_class,
    visc_table,
    multiplier,
    marker_cell,
    marker_frac,
    pair_sphere,
    pair_partner,
    pair_normal,
    pair_gap,
    contact_force,
):
    comps, bx, by, depth = velocity.shape
    spheres, markers = marker_cell.shape
    pairs = pair_sphere.shape[0]
    dims = (bx, by, depth)
    own = bx * by
    count = (bx + 1) * by + 16
    padded = -(-comps * count // 16) * 16
    long = ROWS * (bx + LO + HI + 2)
    edge = comps * HI + comps * 2
    vel = velocity.reshape(comps, own, depth)
    force = force.reshape(comps, own, depth)
    vclass = visc_class.reshape(own, depth)
    sphere = pair_sphere.reshape(1, pairs)
    partner = pair_partner.reshape(1, pairs)
    gap = pair_gap.reshape(1, pairs)
    contact = contact_force.reshape(1, pairs)

    total = (padded, depth)
    ext = (2 * comps, long, depth)
    ext_mu = (2 * comps + 1, long, depth)
    mid = (comps, long, depth)
    coef = (6, long, depth)
    stack = (padded, depth)
    marks = (comps, spheres, markers)
    rows = (comps, count, depth)
    field = (comps, own, depth)
    strips = (edge + 1 + HI, bx, depth)
    planes = (edge + HI, ROWS, depth)

    ints = functools.partial(jax.ShapeDtypeStruct, dtype=jnp.int32)
    first, second, rhs, mu, plane, deep, vel, force, mult, *pair = call(
        functools.partial(first_kernel, dims, count),
        "spread_first",
        [vel, force, vclass, visc_table, multiplier, marker_cell, marker_frac]
        + [sphere, partner, pair_normal, gap, contact],
        [strips, strips, rows, (own, depth), (count, spheres * markers)]
        + [jax.ShapeDtypeStruct((2 * depth, spheres * markers), BF16), field, field, marks]
        + [ints((1, pairs)), ints((1, pairs)), (comps, pairs), (1, pairs), (1, pairs)],
        [
            pltpu.VMEM((own, depth), jnp.int32),
            pltpu.SMEM(visc_table.shape, F32),
            pltpu.VMEM((spheres, markers), jnp.int32),
            marks,
            total,
            pltpu.SemaphoreType.DMA((12,)),
        ],
        hbm=True,
    )
    sphere, partner, normal, gap, contact = pair
    (means,) = call(mean_kernel, "means", [plane, deep], [(spheres, count, depth)])
    near = swap(first, second, 1)
    first, second = call(
        functools.partial(pack_kernel, dims, True),
        "pack_first",
        [*near, vel, rhs, mu],
        [planes, planes],
    )
    far = swap(first, second, 0)
    strips = (edge + 2, bx, depth)
    planes = (edge + 2, ROWS, depth)
    first, second, vel, rhs, mu, mult, sv = call(
        functools.partial(middle_kernel, dims),
        "iterate",
        [*near, *far, vel, mu, rhs, force, mult, plane, deep, sphere, normal, contact],
        [strips, strips, field, rows, (long, depth), marks, (8, depth)],
        [ext_mu, mid, coef, stack, marks, total],
    )
    near = swap(first, second, 1)
    first, second = call(
        functools.partial(pack_kernel, dims, False),
        "pack_second",
        [*near, vel, rhs, sv],
        [planes, planes],
    )
    far = swap(first, second, 0)
    stacked, contact, sv = call(
        functools.partial(last_kernel, dims),
        "finish",
        [*near, *far, sv, vel, mu, rhs, means, sphere, partner, normal, gap, contact],
        [stack, (1, pairs), (8, depth)],
        [ext, mid, coef],
    )
    near = swap(sv, sv, 1)
    vel, mult = call(
        functools.partial(marker_kernel, dims),
        "markers",
        [stacked, plane, deep, mult, sv],
        [field, marks],
        [marks],
    )
    (three,) = call(gather_kernel, "gather", [*near, sv], [(24, depth)])
    far = swap(three, three, 0)
    (contact,) = call(
        functools.partial(contact_kernel, comps, spheres),
        "contact",
        [three, *far, sphere, partner, normal, gap, contact],
        [(1, pairs)],
    )
    return (vel.reshape(comps, bx, by, depth), mult, contact.reshape(pairs))


def solution(mesh):
    in_specs = (
        P(None, "wide", "narrow", None),
        P(None, "wide", "narrow", None),
        P("wide", "narrow", None),
        P(),
        P(None, ("wide", "narrow"), None),
        P(("wide", "narrow"), None),
        P(None, ("wide", "narrow"), None),
        P(("wide", "narrow")),
        P(("wide", "narrow")),
        P(None, ("wide", "narrow")),
        P(("wide", "narrow")),
        P(("wide", "narrow")),
    )
    out_specs = (
        P(None, "wide", "narrow", None),
        P(None, ("wide", "narrow"), None),
        P(("wide", "narrow")),
    )
    return jax.shard_map(local, mesh=mesh, in_specs=in_specs, out_specs=out_specs, check_vma=False)
```

```python
import functools

import jax
import jax.numpy as jnp
from jax import lax
from jax.experimental import pallas as pl
from jax.experimental.pallas import tpu as pltpu
from jax.sharding import PartitionSpec as P

ITERS = 2
SWEEPS = 2

base_diag = 1.0
spread_gain = 0.25
rigid_step = 0.5
contact_step = 0.5
contact_gain = 0.5

F32 = jnp.float32
BF16 = jnp.bfloat16

LO = SWEEPS
HI = SWEEPS + 1
ROWS = 16
CHUNK = 1024
GRANT = 16 * 1024 * 1024


def swaps(along, axes, sizes):
    across = 1 - along
    lists = []
    for kind in (1, 0):
        pairs = []
        for wide in range(sizes[0]):
            for narrow in range(sizes[1]):
                here = [wide, narrow]
                there = list(here)
                spot = here[along]
                there[along] = spot ^ 1 if kind == 0 else ((spot + 1) ^ 1) - 1
                if not 0 <= there[along] < sizes[along]:
                    there = list(here)
                    there[across] = here[across] ^ 1
                    if there[across] >= sizes[across]:
                        continue
                pairs.append((here[0] * sizes[1] + here[1], there[0] * sizes[1] + there[1]))
        lists.append((kind, pairs))
    return lists


def swap(first, second, along):
    axes = ("wide", "narrow")
    sizes = (lax.axis_size("wide"), lax.axis_size("narrow"))
    got = {}
    for kind, pairs in swaps(along, axes, sizes):
        got[kind] = lax.ppermute(first if kind == 0 else second, axes, pairs)
    return got[0], got[1]


class Side:
    def __init__(self, axis):
        self.spot = lax.axis_index(axis)
        self.even = lax.rem(self.spot, 2) == 0
        self.has_down = self.spot > 0
        self.has_up = self.spot < lax.axis_size(axis) - 1

    def emit(self, write, first, second):
        @pl.when(self.even)
        def _():
            write(first, second)

        @pl.when(jnp.logical_not(self.even))
        def _():
            write(second, first)

    def down(self, first, second, block):
        got = jnp.where(self.even, second[block], first[block])
        return jnp.where(self.has_down, got, F32(0.0))

    def up(self, first, second, block):
        got = jnp.where(self.even, first[block], second[block])
        return jnp.where(self.has_up, got, F32(0.0))


def zrow(x, y):
    return ROWS * (x + LO + 1) + y + LO


def hat(position, count):
    ids = lax.broadcasted_iota(jnp.int32, (count, position.shape[1]), 0).astype(F32)
    return jnp.maximum(F32(0.0), 1.0 - jnp.abs(ids - position))


def parts(value):
    high = value.astype(BF16)
    return high, (value - high.astype(F32)).astype(BF16)


def geometry(cell_ref, frac_ref, s, start, span, plane, deep, dims):
    bx, by, depth = dims
    markers = cell_ref.shape[1]
    at = pl.ds(start, span)
    to = pl.ds(s * markers + start, span)
    cell = cell_ref[s : s + 1, at]
    z_bits, y_bits = depth.bit_length() - 1, by.bit_length() - 1
    cz = cell & (depth - 1)
    cy = (cell >> z_bits) & (by - 1)
    cx = cell >> (z_bits + y_bits)
    wx = hat(cx.astype(F32) + frac_ref[0, s : s + 1, at], 16)
    wy = hat(cy.astype(F32) + frac_ref[1, s : s + 1, at], 16)
    for x in range(bx + 1):
        plane[x * by : (x + 1) * by, to] = wx[x : x + 1] * wy[0:by]
    plane[(bx + 1) * by :, to] = wx * wy[by : by + 1]
    high, low = parts(hat(cz.astype(F32) + frac_ref[2, s : s + 1, at], depth))
    deep[0:depth, to] = high
    deep[depth : 2 * depth, to] = low


def chunks(spheres, markers):
    span = min(CHUNK, markers)
    return [(s, start, span) for s in range(spheres) for start in range(0, markers, span)]


def weighted(rows, deep):
    both = lax.dot_general(
        jnp.concatenate(parts(rows), axis=0),
        deep,
        (((1,), (1,)), ((), ())),
        preferred_element_type=F32,
    )
    count, half = rows.shape[0], both.shape[1] // 2
    both = both[:count] + both[count:]
    return both[:, :half] + both[:, half:]


def spread(mult_ref, plane, deep, force_ref, total, out_ref, dims, prepare=None):
    bx, by, depth = dims
    comps, spheres, markers = mult_ref.shape
    count = plane.shape[0]
    for k, (s, start, span) in enumerate(chunks(spheres, markers)):
        if prepare is not None:
            prepare(s, start, span)
        at = pl.ds(s * markers + start, span)
        weights = plane[:, at]
        rows = [
            weights * (spread_gain * mult_ref[c, s : s + 1, pl.ds(start, span)])
            for c in range(comps)
        ]
        rest = total.shape[0] - comps * count
        if rest:
            rows.append(jnp.zeros((rest, span), F32))
        add = weighted(jnp.concatenate(rows, axis=0), deep[:, at])
        if k:
            total[...] += add
        else:
            total[...] = add
    own = bx * by
    for c in range(comps):
        part = total[c * count : (c + 1) * count, :]
        out_ref[c, :own, :] = part[:own] + force_ref[c]
        out_ref[c, own:, :] = part[own:]


def stack_up(vel, stack, dims):
    bx, by, _ = dims
    tail = (bx + 1) * by
    stack[:, tail:, :] = jnp.zeros((stack.shape[0], stack.shape[1] - tail, stack.shape[2]), F32)
    for c in range(stack.shape[0]):
        for x in range(bx + 1):
            at = zrow(x, 0)
            stack[c, x * by : (x + 1) * by, :] = vel[c, at : at + by, :]
            at = zrow(x, by)
            stack[c, tail + x : tail + x + 1, :] = vel[c, at : at + 1, :]


def sample(stack, plane, deep, mv):
    comps, spheres, markers = mv.shape
    count = plane.shape[0]
    rows = [stack[c] for c in range(comps)]
    rest = -comps * count % 16
    if rest:
        rows.append(jnp.zeros((rest, stack.shape[2]), F32))
    high, low = parts(jnp.concatenate(rows, axis=0))
    lhs = jnp.concatenate([high, high, low, low], axis=1)
    for s, start, span in chunks(spheres, markers):
        at = pl.ds(s * markers + start, span)
        weights = deep[:, at]
        near = jnp.dot(
            lhs, jnp.concatenate([weights, weights], axis=0), preferred_element_type=F32
        )
        for c in range(comps):
            mv[c, s : s + 1, pl.ds(start, span)] = jnp.sum(
                near[c * count : (c + 1) * count] * plane[:, at], axis=0, keepdims=True
            )


class Plan:
    def __init__(self, comps, dims, first_round):
        bx, by, _ = dims
        self.comps, self.bx, self.by = comps, bx, by
        self.known = not first_round
        self.mu = 2 * comps
        deep = list(range(comps)) + ([self.mu] if first_round else [])
        rhs = list(range(comps, 2 * comps))
        skip = 1 if self.known else 0
        self.strips_up = [(f, by - LO + i) for f in deep for i in range(LO)]
        self.strips_down = [(f, i) for f in deep for i in range(skip, HI)]
        self.strips_up += [(f, y) for f in rhs for y in (by - 1, by)]
        self.strips_down += [(f, y) for f in rhs for y in (0, 1)]
        self.blocks_up = [(f, bx - LO + i) for f in deep for i in range(LO)]
        self.blocks_down = [(f, i) for f in deep for i in range(skip, HI)]
        self.blocks_up += [(f, x) for f in rhs for x in (bx - 1, bx)]
        self.blocks_down += [(f, x) for f in rhs for x in (0, 1)]
        self.rows_up, self.rows_down = [], []
        for f in deep:
            for i in range(LO):
                far = LO - 1 - i
                reach = LO - 1 - far
                ys = list(range(-reach, 0)) + list(range(by, by + 1 + reach))
                self.rows_up += [(f, bx - LO + i, y) for y in ys]
            for i in range(HI):
                reach = LO - i
                ys = list(range(-reach, 0)) + list(range(by, by + 1 + reach))
                if self.known and i == 0:
                    ys.remove(by)
                self.rows_down += [(f, i, y) for y in ys]
        for f in rhs:
            self.rows_up += [(f, bx - 1, by)] + [(f, bx, y) for y in (-1, by, by + 1)]
            self.rows_down += [(f, 1, by)] + [(f, 0, y) for y in (-1, by, by + 1)]
        self.edge = max(len(self.strips_up), len(self.strips_down))
        self.narrow_blocks = self.edge + (1 if first_round else 2)
        self.row_block = max(len(self.blocks_up), len(self.blocks_down))
        self.sv_block = self.row_block + -(-max(len(self.rows_up), len(self.rows_down)) // 8)
        self.wide_blocks = self.sv_block + (0 if first_round else 3)


def own_rows(refs, plan, f, x, y=None):
    field = refs[f]
    if y is None:
        return field[x * plan.by : (x + 1) * plan.by, :]
    row = x * plan.by + y if y < plan.by else (plan.bx + 1) * plan.by + x
    return field[row : row + 1, :]


def narrow_payload(up, down, plan, refs, sv):
    bx, by, comps = plan.bx, plan.by, plan.comps
    for part, strips in ((up, plan.strips_up), (down, plan.strips_down)):
        for k, (f, y) in enumerate(strips):
            if y == by:
                part[k] = refs[f][(bx + 1) * by : (bx + 1) * by + bx, :]
            else:
                part[k] = refs[f][pl.ds(y, bx, stride=by), :]
        for k in range(len(strips), plan.edge):
            part[k] = jnp.zeros(part.shape[1:], F32)
        for c in range(comps):
            for i, y in enumerate((by - 1, by) if part is up else (0, 1)):
                part[plan.edge, 2 * c + i : 2 * c + i + 1, :] = own_rows(
                    refs, plan, comps + c, bx, y
                )
        part[plan.edge, 2 * comps :, :] = jnp.zeros((8 - 2 * comps, part.shape[2]), F32)
        if sv is not None:
            part[plan.edge + 1] = sv


def narrow_halo(plan, side, first, second):
    by, comps = plan.by, plan.comps
    got = {}
    low, high = {}, {}
    for k, (f, y) in enumerate(plan.strips_up):
        low[f, y - by] = k
    for k, (f, y) in enumerate(plan.strips_down):
        high[f, y + by] = k

    for which, get, keys in (("down", side.down, low), ("up", side.up, high)):
        for k in [*keys.values(), plan.edge]:
            got[which, k] = get(first, second, k)

    def halo(f, y, x=None):
        which, k = ("down", low[f, y]) if y < 1 else ("up", high[f, y])
        if x is None:
            return got[which, k]
        if x == plan.bx:
            spot = 2 * (f - comps) + (y + 1 if y < 1 else y - by)
            return got[which, plan.edge][spot : spot + 1]
        return got[which, k][x : x + 1]

    return halo


def first_kernel(dims, plan, *refs):
    ins, outs, scratch = refs[:12], refs[12:26], refs[26:]
    vel, force, vclass, table, mult, cell, frac = ins[:7]
    first, second, rhs, mu, plane, deep, vel_out, force_out, mult_out = outs[:9]
    class_here, table_here, cell_here, frac_here, total, sems = scratch
    copies = [
        pltpu.make_async_copy(source, target, sems.at[i])
        for i, (source, target) in enumerate(
            [
                (cell, cell_here),
                (frac, frac_here),
                (mult, mult_out),
                (force, force_out),
                (table, table_here),
                (vclass, class_here),
                (vel, vel_out),
            ]
            + list(zip(ins[7:], outs[9:]))
        )
    ]
    for copy in copies:
        copy.start()
    for copy in copies[:4]:
        copy.wait()

    def prepare(s, start, span):
        geometry(cell_here, frac_here, s, start, span, plane, deep, dims)

    spread(mult_out, plane, deep, force_out, total, rhs, dims, prepare)
    for copy in copies[4:]:
        copy.wait()
    value = jnp.zeros(class_here.shape, F32)
    for k in range(table.shape[0]):
        value = value + jnp.where(class_here[...] == k, table_here[k], F32(0.0))
    mu[...] = value
    fields = [ref.at[c] for ref in (vel_out, rhs) for c in range(plan.comps)] + [mu]
    Side("narrow").emit(
        lambda up, down: narrow_payload(up, down, plan, fields, None), first, second
    )


def mean_kernel(plane, deep, out):
    spheres, count, _ = out.shape
    markers = plane.shape[1] // spheres
    for s in range(spheres):
        at = pl.ds(s * markers, markers)
        rows = plane[:, at]
        rest = -count % 16
        if rest:
            rows = jnp.concatenate([rows, jnp.zeros((rest, markers), F32)], axis=0)
        out[s] = weighted(rows, deep[:, at])[:count] * (1.0 / markers)


def pack_kernel(plan, got_a, got_b, vel, rhs, extra, first, second):
    narrow, wide = Side("narrow"), Side("wide")
    comps, by = plan.comps, plan.by
    halo = narrow_halo(plan, narrow, got_a, got_b)
    refs = [vel.at[c] for c in range(comps)] + [rhs.at[c] for c in range(comps)] + [extra]
    zero = jnp.zeros(first.shape[1:], F32)

    def row(f, x, y):
        is_rhs = comps <= f < 2 * comps
        if is_rhs and y == by:
            return own_rows(refs, plan, f, x, y) + halo(f, y, x)
        if plan.known and not is_rhs and y == by:
            return own_rows(refs, plan, f, x, y)
        return halo(f, y, x)

    def fill(part, blocks, rows):
        for k, (f, x) in enumerate(blocks):
            part[k] = own_rows(refs, plan, f, x)
            if comps <= f < 2 * comps:
                part[k, 0:1, :] += halo(f, 0, x)
        for k in range(len(blocks), plan.row_block):
            part[k] = zero
        for k in range(plan.row_block + len(rows) // 8, plan.sv_block):
            part[k] = zero
        for i, (f, x, y) in enumerate(rows):
            part[plan.row_block + i // 8, i % 8 : i % 8 + 1, :] = row(f, x, y)
        if plan.known:
            part[plan.sv_block] = narrow.down(got_a, got_b, plan.edge + 1)
            part[plan.sv_block + 1] = extra[...]
            part[plan.sv_block + 2] = narrow.up(got_a, got_b, plan.edge + 1)

    def write(up, down):
        fill(up, plan.blocks_up, plan.rows_up)
        fill(down, plan.blocks_down, plan.rows_down)

    wide.emit(write, first, second)


def assemble(plan, vel, mu, rhs, near, far, narrow, wide, ext):
    bx, by, comps = plan.bx, plan.by, plan.comps
    halo = narrow_halo(plan, narrow, *near)
    refs = [vel.at[c] for c in range(comps)] + [rhs.at[c] for c in range(comps)] + [mu]

    def column(y):
        return pl.ds(zrow(0, y), bx, stride=ROWS)

    for f in range(ext.shape[0]):
        is_rhs = comps <= f < 2 * comps
        ext[f] = jnp.zeros(ext.shape[1:], F32)
        past = is_rhs or (plan.known and f < comps)
        for x in range(bx + 1 if past else bx):
            ext[f, zrow(x, 0) : zrow(x, by), :] = own_rows(refs, plan, f, x)
        tail = (bx + 1) * by
        if is_rhs:
            ext[f, column(-1), :] = halo(f, -1)
            ext[f, column(0), :] += halo(f, 0)
            ext[f, column(by), :] = refs[f][tail : tail + bx, :] + halo(f, by)
            ext[f, column(by + 1), :] = halo(f, by + 1)
            for y in (-1, 0, by, by + 1):
                got = halo(f, y, bx)
                if y in (0, by):
                    got = got + own_rows(refs, plan, f, bx, y)
                ext[f, zrow(bx, y) : zrow(bx, y) + 1, :] = got
            continue
        if past:
            ext[f, column(by), :] = refs[f][tail : tail + bx, :]
            ext[f, zrow(bx, by) : zrow(bx, by) + 1, :] = own_rows(refs, plan, f, bx, by)
        for y in list(range(-LO, 0)) + list(range(by + 1 if past else by, by + HI)):
            ext[f, column(y), :] = halo(f, y)
    for get, shift, blocks, rows in (
        (wide.down, -bx, plan.blocks_up, plan.rows_up),
        (wide.up, bx, plan.blocks_down, plan.rows_down),
    ):
        for k, (f, x) in enumerate(blocks):
            x = x + shift
            at = pl.ds(zrow(x, 0), by)
            got = get(*far, k)
            if comps <= f < 2 * comps and x in (0, bx):
                ext[f, at, :] += got
            else:
                ext[f, at, :] = got
        for i, (f, x, y) in enumerate(rows):
            x = x + shift
            at = pl.ds(zrow(x, y), 1)
            if i % 8 == 0:
                block = get(*far, plan.row_block + i // 8)
            got = block[i % 8 : i % 8 + 1]
            if comps <= f < 2 * comps and x in (0, bx):
                ext[f, at, :] += got
            else:
                ext[f, at, :] = got


def sweeps(dims, comps, mu, narrow, wide, ext, mid, coef):
    bx, by, depth = dims
    shape = (ROWS, depth)
    lane = lax.broadcasted_iota(jnp.int32, shape, 1)
    row = lax.broadcasted_iota(jnp.int32, shape, 0) - LO
    inside_y = jnp.logical_and(
        jnp.logical_or(row >= 0, narrow.has_down), jnp.logical_or(row < by, narrow.has_up)
    )
    first, last = lane == 0, lane == depth - 1

    def at(x, shift=0):
        return pl.ds(zrow(x, -LO) + shift, ROWS)

    for x in range(-LO + 1, bx + HI - 1):
        here = mu[at(x), :]
        down_x = 0.5 * (here + mu[at(x - 1), :])
        up_x = 0.5 * (here + mu[at(x + 1), :])
        down_y = 0.5 * (here + mu[at(x, -1), :])
        up_y = 0.5 * (here + mu[at(x, 1), :])
        down_z = 0.5 * (here + jnp.where(first, 0.0, pltpu.roll(here, 1, 1)))
        up_z = 0.5 * (here + jnp.where(last, 0.0, pltpu.roll(here, depth - 1, 1)))
        diagonal = base_diag + down_x + up_x + down_y + up_y + down_z + up_z
        inside = inside_y
        if x < 0:
            inside = jnp.logical_and(inside, wide.has_down)
        if x >= bx:
            inside = jnp.logical_and(inside, wide.has_up)
        coef[0, at(x), :] = down_x
        coef[1, at(x), :] = down_y
        coef[2, at(x), :] = up_y
        coef[3, at(x), :] = jnp.where(first, 0.0, down_z)
        coef[4, at(x), :] = jnp.where(last, 0.0, up_z)
        coef[5, at(x), :] = jnp.where(inside, 1.0 / diagonal, 0.0)
        if x == bx + HI - 2:
            coef[0, at(x + 1), :] = up_x

    for source, target, span in (
        (ext, mid, range(-1, bx + 2)),
        (mid, ext, range(0, bx + 1)),
    ):
        for x in span:
            down_x, up_x = coef[0, at(x), :], coef[0, at(x + 1), :]
            down_y, up_y = coef[1, at(x), :], coef[2, at(x), :]
            down_z, up_z, inverse = coef[3, at(x), :], coef[4, at(x), :], coef[5, at(x), :]
            for c in range(comps):
                here = source[c, at(x), :]
                value = (
                    ext[comps + c, at(x), :]
                    + down_x * source[c, at(x - 1), :]
                    + up_x * source[c, at(x + 1), :]
                    + down_y * source[c, at(x, -1), :]
                    + up_y * source[c, at(x, 1), :]
                    + down_z * pltpu.roll(here, 1, 1)
                    + up_z * pltpu.roll(here, depth - 1, 1)
                )
                target[c, at(x), :] = value * inverse


def sphere_pushes(sphere, normal, contact, comps, spheres):
    pushes = {}
    for c in range(comps):
        load = normal[c : c + 1, :] * contact
        for s in range(spheres):
            pushes[c, s] = contact_gain * jnp.sum(
                jnp.where(sphere == s, load, 0.0), axis=1, keepdims=True
            )
    return pushes


def move_markers(mult, mv, sv, new_mult):
    comps, spheres, _ = mult.shape
    for c in range(comps):
        for s in range(spheres):
            row = s * comps + c
            new_mult[c, s : s + 1, :] = mult[c, s : s + 1, :] + rigid_step * (
                sv[row : row + 1, 0:1] - mv[c, s : s + 1, :]
            )


def new_contact(blocks, sphere, partner, normal, gap, contact, comps, spheres):
    pairs = contact.shape[1]
    closing = jnp.zeros_like(contact)
    for c in range(comps):
        speed = jnp.zeros_like(contact)
        for q, block in enumerate(blocks):
            for s in range(spheres):
                line = block[s * comps + c : s * comps + c + 1, :pairs]
                speed = speed + jnp.where(partner == q * spheres + s, line, 0.0)
        own = jnp.zeros_like(contact)
        for s in range(spheres):
            line = blocks[4][s * comps + c : s * comps + c + 1, :pairs]
            own = own + jnp.where(sphere == s, line, 0.0)
        closing = closing + normal[c : c + 1, :] * (speed - own)
    return jnp.maximum(0.0, contact - contact_step * (gap + closing))


def middle_kernel(
    dims, plan, next_plan,
    near_a, near_b, far_a, far_b,
    vel, mu, rhs, force, mult, plane, deep, sphere, normal, contact,
    first, second, stack, rhs_out, mu_out, mult_out, sv,
    ext, mid, coef, mv, total,
):
    comps, spheres, markers = mult.shape
    narrow, wide = Side("narrow"), Side("wide")
    assemble(plan, vel, mu, rhs, (near_a, near_b), (far_a, far_b), narrow, wide, ext)
    mu_out[...] = ext[2 * comps]
    sweeps(dims, comps, ext.at[2 * comps], narrow, wide, ext, mid, coef)
    stack_up(ext, stack, dims)
    sample(stack, plane, deep, mv)
    pushes = sphere_pushes(sphere[...], normal, contact[...], comps, spheres)
    sv[...] = jnp.zeros_like(sv)
    for c in range(comps):
        mean = jnp.sum(mv[c], axis=1, keepdims=True) / markers
        for s in range(spheres):
            row = s * comps + c
            sv[row : row + 1, :] = jnp.broadcast_to(
                mean[s : s + 1] + pushes[c, s], (1, sv.shape[1])
            )
    move_markers(mult, mv, sv, mult_out)
    spread(mult_out, plane, deep, force, total, rhs_out, dims)
    fields = [ref.at[c] for ref in (stack, rhs_out) for c in range(comps)]
    narrow.emit(
        lambda up, down: narrow_payload(up, down, next_plan, fields, sv[...]), first, second
    )


def last_kernel(
    dims, plan,
    near_a, near_b, far_a, far_b, old_sv,
    vel, mu, rhs, means, sphere, partner, normal, gap, contact,
    stack, contact_out, sv,
    ext, mid, coef,
):
    comps = vel.shape[0]
    spheres = means.shape[0]
    narrow, wide = Side("narrow"), Side("wide")
    assemble(plan, vel, None, rhs, (near_a, near_b), (far_a, far_b), narrow, wide, ext)
    sweeps(dims, comps, mu, narrow, wide, ext, mid, coef)
    stack_up(ext, stack, dims)
    blocks = [
        get(far_a, far_b, plan.sv_block + i) for get in (wide.down, wide.up) for i in range(3)
    ]
    blocks[3:3] = [
        narrow.down(near_a, near_b, plan.edge + 1),
        old_sv[...],
        narrow.up(near_a, near_b, plan.edge + 1),
    ]
    now = new_contact(
        blocks, sphere[...], partner[...], normal, gap[...], contact[...], comps, spheres
    )
    contact_out[...] = now
    pushes = sphere_pushes(sphere[...], normal, now, comps, spheres)
    sv[...] = jnp.zeros_like(sv)
    for c in range(comps):
        for s in range(spheres):
            row = s * comps + c
            mean = jnp.sum(
                jnp.sum(stack[c] * means[s], axis=0, keepdims=True), axis=1, keepdims=True
            )
            sv[row : row + 1, :] = jnp.broadcast_to(mean + pushes[c, s], (1, sv.shape[1]))


def marker_kernel(dims, stack, plane, deep, mult, sv, vel_out, mult_out, mv):
    bx, by, _ = dims
    for c in range(mult.shape[0]):
        vel_out[c] = stack[c, : bx * by, :]
    sample(stack, plane, deep, mv)
    move_markers(mult, mv, sv, mult_out)


def gather_kernel(got_a, got_b, sv, out):
    narrow = Side("narrow")
    every = slice(None)
    out[0:8, :] = narrow.down(got_a, got_b, every)
    out[8:16, :] = sv[...]
    out[16:24, :] = narrow.up(got_a, got_b, every)


def contact_kernel(comps, spheres, own, got_a, got_b, sphere, partner, normal, gap, contact, out):
    wide = Side("wide")
    every = slice(None)
    blocks = []
    for part in (wide.down(got_a, got_b, every), own[...], wide.up(got_a, got_b, every)):
        blocks += [part[0:8], part[8:16], part[16:24]]
    out[...] = new_contact(
        blocks, sphere[...], partner[...], normal, gap[...], contact[...], comps, spheres
    )


def call(kernel, name, ins, outs, scratch=(), hbm=False):
    vmem = pl.BlockSpec(memory_space=pltpu.VMEM)
    apart = pl.BlockSpec(memory_space=pltpu.HBM)
    outs = [out if isinstance(out, jax.ShapeDtypeStruct) else jax.ShapeDtypeStruct(out, F32) for out in outs]
    if hbm:
        ins = [pltpu.with_memory_space_constraint(x, pltpu.HBM) for x in ins]
    return pl.pallas_call(
        kernel,
        name=name,
        in_specs=[apart if hbm else vmem] * len(ins),
        out_specs=[vmem] * len(outs),
        out_shape=outs,
        scratch_shapes=[
            pltpu.VMEM(shape, F32) if isinstance(shape, tuple) else shape for shape in scratch
        ],
        compiler_params=pltpu.CompilerParams(vmem_limit_bytes=GRANT),
    )(*ins)


def local(
    velocity,
    force,
    visc_class,
    visc_table,
    multiplier,
    marker_cell,
    marker_frac,
    pair_sphere,
    pair_partner,
    pair_normal,
    pair_gap,
    contact_force,
):
    comps, bx, by, depth = velocity.shape
    spheres, markers = marker_cell.shape
    pairs = pair_sphere.shape[0]
    dims = (bx, by, depth)
    own = bx * by
    count = (bx + 1) * by + 16
    padded = -(-comps * count // 16) * 16
    long = ROWS * (bx + LO + HI + 2)
    plans = [Plan(comps, dims, first_round) for first_round in (True, False)]
    vel = velocity.reshape(comps, own, depth)
    force = force.reshape(comps, own, depth)
    vclass = visc_class.reshape(own, depth)
    sphere = pair_sphere.reshape(1, pairs)
    partner = pair_partner.reshape(1, pairs)
    gap = pair_gap.reshape(1, pairs)
    contact = contact_force.reshape(1, pairs)

    total = (padded, depth)
    ext = (2 * comps, long, depth)
    ext_mu = (2 * comps + 1, long, depth)
    mid = (comps, long, depth)
    coef = (6, long, depth)
    marks = (comps, spheres, markers)
    rows = (comps, count, depth)
    field = (comps, own, depth)
    strips = [(plan.narrow_blocks, bx, depth) for plan in plans]
    planes = [(plan.wide_blocks, by, depth) for plan in plans]

    ints = functools.partial(jax.ShapeDtypeStruct, dtype=jnp.int32)
    first, second, rhs, mu, plane, deep, vel, force, mult, *pair = call(
        functools.partial(first_kernel, dims, plans[0]),
        "spread_first",
        [vel, force, vclass, visc_table, multiplier, marker_cell, marker_frac]
        + [sphere, partner, pair_normal, gap, contact],
        [strips[0], strips[0], rows, (own, depth), (count, spheres * markers)]
        + [jax.ShapeDtypeStruct((2 * depth, spheres * markers), BF16), field, field, marks]
        + [ints((1, pairs)), ints((1, pairs)), (comps, pairs), (1, pairs), (1, pairs)],
        [
            pltpu.VMEM((own, depth), jnp.int32),
            pltpu.SMEM(visc_table.shape, F32),
            pltpu.VMEM((spheres, markers), jnp.int32),
            marks,
            total,
            pltpu.SemaphoreType.DMA((12,)),
        ],
        hbm=True,
    )
    sphere, partner, normal, gap, contact = pair
    (means,) = call(mean_kernel, "means", [plane, deep], [(spheres, count, depth)])
    near = swap(first, second, 1)
    first, second = call(
        functools.partial(pack_kernel, plans[0]),
        "pack_first",
        [*near, vel, rhs, mu],
        [planes[0], planes[0]],
    )
    far = swap(first, second, 0)
    first, second, vel, rhs, mu, mult, sv = call(
        functools.partial(middle_kernel, dims, *plans),
        "iterate",
        [*near, *far, vel, mu, rhs, force, mult, plane, deep, sphere, normal, contact],
        [strips[1], strips[1], rows, rows, (long, depth), marks, (8, depth)],
        [ext_mu, mid, coef, marks, total],
    )
    near = swap(first, second, 1)
    first, second = call(
        functools.partial(pack_kernel, plans[1]),
        "pack_second",
        [*near, vel, rhs, sv],
        [planes[1], planes[1]],
    )
    far = swap(first, second, 0)
    stacked, contact, sv = call(
        functools.partial(last_kernel, dims, plans[1]),
        "finish",
        [*near, *far, sv, vel, mu, rhs, means, sphere, partner, normal, gap, contact],
        [rows, (1, pairs), (8, depth)],
        [ext, mid, coef],
    )
    near = swap(sv, sv, 1)
    vel, mult = call(
        functools.partial(marker_kernel, dims),
        "markers",
        [stacked, plane, deep, mult, sv],
        [field, marks],
        [marks],
    )
    (three,) = call(gather_kernel, "gather", [*near, sv], [(24, depth)])
    far = swap(three, three, 0)
    (contact,) = call(
        functools.partial(contact_kernel, comps, spheres),
        "contact",
        [three, *far, sphere, partner, normal, gap, contact],
        [(1, pairs)],
    )
    return (vel.reshape(comps, bx, by, depth), mult, contact.reshape(pairs))


def solution(mesh):
    in_specs = (
        P(None, "wide", "narrow", None),
        P(None, "wide", "narrow", None),
        P("wide", "narrow", None),
        P(),
        P(None, ("wide", "narrow"), None),
        P(("wide", "narrow"), None),
        P(None, ("wide", "narrow"), None),
        P(("wide", "narrow")),
        P(("wide", "narrow")),
        P(None, ("wide", "narrow")),
        P(("wide", "narrow")),
        P(("wide", "narrow")),
    )
    out_specs = (
        P(None, "wide", "narrow", None),
        P(None, ("wide", "narrow"), None),
        P(("wide", "narrow")),
    )
    return jax.shard_map(local, mesh=mesh, in_specs=in_specs, out_specs=out_specs, check_vma=False)
```
